32 devices in a mesh: dp: 16 (over z, y, core), tensor: 2 (over x).
Axes of the slice: x: 2, y: 2, z: 4, core: 2. Of those that a mesh axis runs over, the one named last changes fastest.
Arguments:
- frames: bfloat16 [16384, 2048], P('dp', 'tensor'), may hold values from -16 to 16
- gain: bfloat16 [2048], P('tensor'), may hold values from 0.099609375 to 1.8984375
- w_first: bfloat16 [32, 64, 128], P('tensor'), may hold values from -0.75 to 0.75
- w_second: bfloat16 [128, 32, 64], P('tensor'), may hold values from -1 to 1
- w_third: bfloat16 [128, 64, 32], P('tensor'), may hold values from -0.75 to 0.75
- w_fourth: bfloat16 [32, 128, 64], P('tensor'), may hold values from -0.5 to 0.5
- cotangent: bfloat16 [16384, 2048], P('dp', 'tensor'), may hold values from -6 to 6
Outputs:
- output: bfloat16 [16384, 2048], P('dp', 'tensor')
- input_gradient: bfloat16 [16384, 2048], P('dp', 'tensor')
- grad_first: float32 [32, 64, 128], P('tensor')
- grad_second: float32 [128, 32, 64], P('tensor')
- grad_third: float32 [128, 64, 32], P('tensor')
- grad_fourth: float32 [32, 128, 64], P('tensor')
- grad_gain: float32 [2048], P('tensor')
The draws below stay inside these ranges and needn't reach their ends.
All inputs are finite; a program needn't handle non-finite values.
Results may differ from the reference program's by a relative error of at most 0.0072.
Values may be sent and summed in bfloat16 or wider, within the bound.
A program may use at most 128 MiB of HBM per device.

```python
import math
import jax
import jax.numpy as jnp
from jax import lax

WIDTH_BLOCK_COUNT = 32
BLOCK_FEATURES = 64
NM = 128
NQ = 64
TOK_DEV = 1024
MODEL_WIDTH = 2048
TOKENS = 16384


def draw_frames(key, part):
    keys = jax.random.split(jax.random.fold_in(key, 17), 3)
    position = jnp.arange(MODEL_WIDTH, dtype=jnp.float32) / (MODEL_WIDTH - 1)
    column = 0.3 * jnp.exp(position * math.log(10.0)) * jnp.exp(jax.random.uniform(keys[1], (MODEL_WIDTH,), jnp.float32, -0.2, 0.2))
    base = jax.random.truncated_normal(keys[0], -3.0, 3.0, (TOKENS, MODEL_WIDTH), jnp.float32)
    row = jnp.exp(jax.random.uniform(keys[2], (TOKENS, 1), jnp.float32, math.log(0.7), math.log(1.4)))
    return (base * column * row).astype(jnp.bfloat16)


def steps_of(rng, shape, pieces, least, top_value):
    level = 1.0
    for dim, parts in pieces:
        steps = jax.random.uniform(jax.random.fold_in(jax.random.fold_in(rng, 6), dim), (parts,), jnp.float32, least / len(pieces), top_value / len(pieces))
        level = level * jnp.repeat(jnp.exp(steps), shape[dim] // parts).reshape((-1,) + (1,) * (len(shape) - 1 - dim))
    return level


def bell_draw(rng, dims, scale, reach, cuts=(), held_as=jnp.bfloat16):
    loudness = steps_of(rng, dims, cuts, -0.22, 0.18) if cuts else 1.0
    result = jax.random.normal(rng, dims, jnp.float32) * scale * loudness
    return jnp.minimum(jnp.maximum(result, -reach), reach).astype(held_as)


def setup_inputs(seed: int = 0) -> dict:
    key_list = jax.random.split(jax.random.key(seed), 8)
    return {
        "frames": draw_frames(jax.random.fold_in(key_list[7], 71), 0),
        "gain": jnp.clip(1.0 + 0.18 * jax.random.normal(key_list[1], (MODEL_WIDTH,), jnp.float32), 0.099609375, 1.8984375).astype(jnp.bfloat16),
        "w_first": bell_draw(key_list[2], (WIDTH_BLOCK_COUNT, BLOCK_FEATURES, NM), BLOCK_FEATURES ** -0.5, 0.75, ((0, 2),)),
        "w_second": bell_draw(key_list[3], (NM, WIDTH_BLOCK_COUNT, NQ), WIDTH_BLOCK_COUNT ** -0.5, 1.0, ((0, 2),)),
        "w_third": bell_draw(key_list[4], (NM, NQ, WIDTH_BLOCK_COUNT), NQ ** -0.5, 0.75, ((0, 2),)),
        "w_fourth": bell_draw(key_list[5], (WIDTH_BLOCK_COUNT, NM, BLOCK_FEATURES), NM ** -0.5, 0.5, ((0, 2),)),
        "cotangent": bell_draw(key_list[6], (TOKENS, MODEL_WIDTH), 1.0, 6.0, ((0, 16), (1, 2))),
    }


def gelu_parts(value):
    cdf = 0.5 * (1.0 + jax.scipy.special.erf(value * 0.7071067811865476))
    pdf = jnp.exp(-0.5 * value * value) * 0.3989422804014327
    return (value * cdf, cdf + value * pdf)

def block_pass(xb, block_index_delta, gain, w_first, w_second, w_third, w_fourth):
    single_float = jnp.float32
    frame_row_count = xb.shape[0]
    input_float = xb.astype(single_float)
    gain_wide_float = gain.astype(single_float)
    row_mean_value = lax.optimization_barrier(jnp.sum(input_float, 1, keepdims=True)) / MODEL_WIDTH
    msq = lax.optimization_barrier(jnp.sum(input_float * input_float, 1, keepdims=True)) / MODEL_WIDTH
    inverse_deviation = 1.0 / jnp.sqrt(msq - row_mean_value * row_mean_value + 1e-05)
    centered_input = (input_float - row_mean_value) * inverse_deviation
    normalized_rows = (centered_input * gain_wide_float).astype(jnp.bfloat16).reshape(frame_row_count, WIDTH_BLOCK_COUNT, BLOCK_FEATURES)
    lifted = jnp.einsum('tai,aim->tam', normalized_rows.astype(single_float), w_first.astype(single_float)).astype(jnp.bfloat16)
    mixed = jnp.einsum('tam,maq->tmq', lifted.astype(single_float), w_second.astype(single_float))
    act, slope = gelu_parts(mixed)
    act_b = act.astype(jnp.bfloat16)
    folded = jnp.einsum('tmq,mqp->tmp', act_b.astype(single_float), w_third.astype(single_float)).astype(jnp.bfloat16)
    back = jnp.einsum('tma,ami->tai', folded.astype(single_float), w_fourth.astype(single_float)).reshape(frame_row_count, MODEL_WIDTH)
    output = (input_float + 0.5 * back).astype(jnp.bfloat16)
    dz = (0.5 * block_index_delta.astype(single_float)).astype(jnp.bfloat16).reshape(frame_row_count, WIDTH_BLOCK_COUNT, BLOCK_FEATURES)
    g_fourth = jnp.einsum('tma,tai->ami', folded.astype(single_float), dz.astype(single_float))
    dfold = jnp.einsum('tai,ami->tma', dz.astype(single_float), w_fourth.astype(single_float)).astype(jnp.bfloat16)
    g_third = jnp.einsum('tmq,tmp->mqp', act_b.astype(single_float), dfold.astype(single_float))
    dmix = (jnp.einsum('tmp,mqp->tmq', dfold.astype(single_float), w_third.astype(single_float)) * slope).astype(jnp.bfloat16)
    g_second = jnp.einsum('tam,tmq->maq', lifted.astype(single_float), dmix.astype(single_float))
    dlift = jnp.einsum('tmq,maq->tam', dmix.astype(single_float), w_second.astype(single_float)).astype(jnp.bfloat16)
    g_first = jnp.einsum('tai,tam->aim', normalized_rows.astype(single_float), dlift.astype(single_float))
    dimension_numbers = jnp.einsum('tam,aim->tai', dlift.astype(single_float), w_first.astype(single_float)).reshape(frame_row_count, MODEL_WIDTH)
    gain_gradient = lax.optimization_barrier(jnp.sum(dimension_numbers * centered_input, 0))
    expected_gradient = dimension_numbers * gain_wide_float
    gradient_mean = lax.optimization_barrier(jnp.sum(expected_gradient, 1, keepdims=True)) / MODEL_WIDTH
    gradient_centered_mean = lax.optimization_barrier(jnp.sum(expected_gradient * centered_input, 1, keepdims=True)) / MODEL_WIDTH
    input_gradient = (block_index_delta.astype(single_float) + inverse_deviation * (expected_gradient - gradient_mean - centered_input * gradient_centered_mean)).astype(jnp.bfloat16)
    return (output, input_gradient, (g_first, g_second, g_third, g_fourth, gain_gradient))

def reference(frames, gain, w_first, w_second, w_third, w_fourth, cotangent):
    single_float = jnp.float32
    blocks = TOKENS // TOK_DEV
    xs = frames.reshape(blocks, TOK_DEV, MODEL_WIDTH)
    ds = cotangent.reshape(blocks, TOK_DEV, MODEL_WIDTH)
    start = (jnp.zeros((WIDTH_BLOCK_COUNT, BLOCK_FEATURES, NM), single_float), jnp.zeros((NM, WIDTH_BLOCK_COUNT, NQ), single_float), jnp.zeros((NM, NQ, WIDTH_BLOCK_COUNT), single_float), jnp.zeros((WIDTH_BLOCK_COUNT, NM, BLOCK_FEATURES), single_float), jnp.zeros((MODEL_WIDTH,), single_float))

    def step(carry, pair):
        output, input_gradient, grads = block_pass(pair[0], pair[1], gain, w_first, w_second, w_third, w_fourth)
        carry = tuple((c + g for c, g in zip(carry, grads)))
        return (carry, (output, input_gradient))
    totals, stacked = lax.scan(step, start, (xs, ds))
    scale = 1.0 / math.sqrt(TOKENS)
    output = stacked[0].reshape(TOKENS, MODEL_WIDTH)
    input_gradient = stacked[1].reshape(TOKENS, MODEL_WIDTH)
    return (output, input_gradient, totals[0] * scale, totals[1] * scale, totals[2] * scale, totals[3] * scale, totals[4] * scale)
```

```python
import math

import jax
import jax.numpy as jnp
from jax import lax
from jax.sharding import PartitionSpec as P

F32 = jnp.float32
BF16 = jnp.bfloat16
LANES = 128


def gelu_parts(value):
    cdf = 0.5 * (1.0 + jax.scipy.special.erf(value * 0.7071067811865476))
    pdf = jnp.exp(-0.5 * value * value) * 0.3989422804014327
    return (value * cdf, cdf + value * pdf)


def dot32(spec, a, b):
    return jnp.einsum(spec, a, b, preferred_element_type=F32)


def swap_in(x, n):
    t, d = x.shape
    parts = lax.all_to_all(x.reshape(n, t // n, d), "tensor", 0, 0)
    return jnp.transpose(parts, (0, 2, 1)).reshape(n * d, t // n)


def swap_out(x, n):
    d, t = x.shape
    parts = jnp.transpose(x.reshape(n, d // n, t), (0, 2, 1))
    return lax.all_to_all(parts, "tensor", 0, 0).reshape(n * t, d // n)


def to_rows(g, n):
    b, r, c = g.shape
    k = LANES // c
    g = g.reshape(n, b // n, r, c)
    step = b // n // k
    if k > 1:
        g = jnp.concatenate([g[:, i * step : (i + 1) * step] for i in range(k)], axis=-1)
    return g.reshape(n, step * r, LANES)


def from_rows(rows, b, r, c):
    k = LANES // c
    g = rows.reshape(b // k, r, LANES)
    if k > 1:
        g = jnp.concatenate([g[:, :, i * c : (i + 1) * c] for i in range(k)], axis=0)
    return g


def tensor_sum(rows, n):
    got = lax.all_to_all(rows.astype(BF16), "tensor", 0, 0)
    return jnp.sum(got.astype(F32), 0)


def per_device(frames, gain, w_first, w_second, w_third, w_fourth, cotangent):
    n = lax.axis_size("tensor")
    dp = lax.axis_size("dp")
    a_loc, i_sz, m_sz = w_first.shape
    m_loc, a_sz, q_sz = w_second.shape
    width = a_sz * i_sz
    t_loc = frames.shape[0] // n

    x = swap_in(frames, n)
    w1 = lax.all_gather(w_first, "tensor", axis=0, tiled=True)
    gain_full = lax.all_gather(gain, "tensor", axis=0, tiled=True)
    w2 = lax.all_gather(w_second, "tensor", axis=0, tiled=True)
    cot = swap_in(cotangent, n)
    w3 = lax.all_gather(w_third, "tensor", axis=0, tiled=True)
    w4 = lax.all_gather(w_fourth, "tensor", axis=0, tiled=True)

    xf = x.astype(F32)
    gw = gain_full.astype(F32)[:, None]
    mean = jnp.sum(xf, 0, keepdims=True) / width
    msq = jnp.sum(xf * xf, 0, keepdims=True) / width
    rstd = 1.0 / jnp.sqrt(msq - mean * mean + 1e-05)
    xhat = (xf - mean) * rstd
    normed = (xhat * gw).astype(BF16).reshape(a_sz, i_sz, t_loc)
    lifted = dot32("ait,aim->amt", normed, w1).astype(BF16)
    mixed = dot32("amt,maq->mqt", lifted, w2)
    act, slope = gelu_parts(mixed)
    act = act.astype(BF16)
    folded = dot32("mqt,mqp->mpt", act, w3).astype(BF16)
    back = dot32("mat,ami->ait", folded, w4).reshape(width, t_loc)
    output = swap_out((xf + 0.5 * back).astype(BF16), n)

    dz = (0.5 * cot.astype(F32)).astype(BF16).reshape(a_sz, i_sz, t_loc)
    g4 = tensor_sum(to_rows(dot32("mat,ait->aim", folded, dz), n), n)
    dfold = dot32("ait,ami->mat", dz, w4).astype(BF16)
    g3 = tensor_sum(to_rows(dot32("mqt,mpt->mpq", act, dfold), n), n)
    dmix = (dot32("mpt,mqp->mqt", dfold, w3) * slope).astype(BF16)
    g2 = tensor_sum(to_rows(dot32("amt,mqt->maq", lifted, dmix), n), n)
    dlift = dot32("mqt,maq->amt", dmix, w2).astype(BF16)
    g1 = tensor_sum(to_rows(dot32("ait,amt->aim", normed, dlift), n), n)
    dn = dot32("amt,aim->ait", dlift, w1).reshape(width, t_loc)
    gg = jnp.sum(dn * xhat, 1)
    e = dn * gw
    e_mean = jnp.sum(e, 0, keepdims=True) / width
    ex_mean = jnp.sum(e * xhat, 0, keepdims=True) / width
    dx = (cot.astype(F32) + rstd * (e - e_mean - xhat * ex_mean)).astype(BF16)
    input_gradient = swap_out(dx, n)
    gg = jnp.sum(lax.all_to_all(gg.reshape(n, width // n), "tensor", 0, 0), 0)

    rows = jnp.concatenate([g1, g2, g3, g4, gg.reshape(-1, LANES)], 0)
    total = lax.psum(rows, "dp") * (1.0 / math.sqrt(frames.shape[0] * dp))
    r = g1.shape[0]
    s1 = from_rows(total[:r], a_loc, i_sz, m_sz)
    s2 = from_rows(total[r : 2 * r], m_loc, a_sz, q_sz)
    s3 = jnp.transpose(from_rows(total[2 * r : 3 * r], m_loc, a_sz, q_sz), (0, 2, 1))
    s4 = jnp.transpose(from_rows(total[3 * r : 4 * r], a_loc, i_sz, m_sz), (0, 2, 1))
    sg = total[4 * r :].reshape(-1)
    return (output, input_gradient, s1, s2, s3, s4, sg)


def solution(mesh):
    blocks = P("tensor", None, None)
    rows = P("dp", "tensor")
    return jax.shard_map(
        per_device,
        mesh=mesh,
        in_specs=(rows, P("tensor"), blocks, blocks, blocks, blocks, rows),
        out_specs=(rows, rows, blocks, blocks, blocks, blocks, P("tensor")),
        check_vma=False,
    )
```

```python
import math

import jax
import jax.numpy as jnp
from jax import lax
from jax.experimental import pallas as pl
from jax.experimental.pallas import tpu as pltpu
from jax.sharding import PartitionSpec as P

F32 = jnp.float32
BF16 = jnp.bfloat16
LANES = 128


def gelu_parts(value):
    cdf = 0.5 * (1.0 + jax.scipy.special.erf(value * 0.7071067811865476))
    pdf = jnp.exp(-0.5 * value * value) * 0.3989422804014327
    return (value * cdf, cdf + value * pdf)


def dot32(spec, a, b):
    return jnp.einsum(spec, a, b, preferred_element_type=F32)


def swap_in(x, n):
    t, d = x.shape
    parts = lax.all_to_all(x.reshape(n, t // n, d), "tensor", 0, 0)
    return jnp.transpose(parts, (0, 2, 1)).reshape(n * d, t // n)


def swap_out(x, n):
    d, t = x.shape
    parts = jnp.transpose(x.reshape(n, d // n, t), (0, 2, 1))
    return lax.all_to_all(parts, "tensor", 0, 0).reshape(n * t, d // n)


def to_rows(g, n):
    b, r, c = g.shape
    k = LANES // c
    g = g.reshape(n, b // n, r, c)
    step = b // n // k
    if k > 1:
        g = jnp.concatenate([g[:, i * step : (i + 1) * step] for i in range(k)], axis=-1)
    return g.reshape(n, step * r, LANES)


def from_rows(rows, b, r, c):
    k = LANES // c
    g = rows.reshape(b // k, r, LANES)
    if k > 1:
        g = jnp.concatenate([g[:, :, i * c : (i + 1) * c] for i in range(k)], axis=0)
    return g


def tensor_sum(rows, n):
    got = lax.all_to_all(jnp.concatenate([r.astype(BF16) for r in rows], 1), "tensor", 0, 0)
    return jnp.sum(got.astype(F32), 0)


def reduce_kernel(group, scale, x_ref, o_ref, send1, recv1, acc1, send2, recv2, acc2, send3, recv3, whole, ssem, rsem):
    me = lax.axis_index("dp")
    rows = x_ref.shape[0]
    half, quarter = rows // 2, rows // 4
    part = quarter // group
    d1, d2, d3 = me % 2, (me // 2) % 2, me // 4
    peer1 = me + 1 - 2 * d1
    peer2 = me + 2 - 4 * d2
    others = [((d3 + k) % group, (d3 + group - k) % group) for k in range(1, group)]

    barrier = pltpu.get_barrier_semaphore()
    for peer in [peer1, peer2] + [to * 4 + me % 4 for to, _ in others]:
        pl.semaphore_signal(barrier, inc=1, device_id={"dp": peer}, device_id_type=pl.DeviceIdType.MESH)
    pl.semaphore_wait(barrier, 1 + group)

    def send(src, dst, slot, peer):
        copy = pltpu.make_async_remote_copy(
            src_ref=src,
            dst_ref=dst,
            send_sem=ssem.at[slot],
            recv_sem=rsem.at[slot],
            device_id={"dp": peer},
            device_id_type=pl.DeviceIdType.MESH,
        )
        copy.start()
        return copy

    def window(start, size):
        return pl.ds(pl.multiple_of(start, 16), size)

    send1[...] = x_ref[window((1 - d1) * half, half), :].astype(BF16)
    copy = send(send1, recv1, 0, peer1)
    acc1[...] = x_ref[window(d1 * half, half), :]
    copy.wait()
    acc1[...] += recv1[...].astype(F32)

    send2[...] = acc1[window((1 - d2) * quarter, quarter), :].astype(BF16)
    copy = send(send2, recv2, 1, peer2)
    acc2[...] = acc1[window(d2 * quarter, quarter), :]
    copy.wait()
    acc2[...] += recv2[...].astype(F32)

    send3[...] = acc2[...].astype(BF16)
    copies = []
    for k, (to, _) in enumerate(others):
        copies.append(send(send3.at[window(to * part, part), :], recv3.at[k], 2 + k, to * 4 + me % 4))
    total = acc2[window(d3 * part, part), :]
    for k, copy in enumerate(copies):
        copy.wait()
        total += recv3[k].astype(F32)

    base1 = d1 * half
    base2 = base1 + d2 * quarter
    base3 = base2 + d3 * part
    whole[window(base3, part), :] = total.astype(BF16)
    mine = whole.at[window(base3, part), :]
    copies = []
    for k, (to, _) in enumerate(others):
        copies.append(send(mine, mine, 1 + group + k, to * 4 + me % 4))
    for copy in copies:
        copy.wait()
    mine = whole.at[window(base2, quarter), :]
    send(mine, mine, 2 * group, peer2).wait()
    mine = whole.at[window(base1, half), :]
    send(mine, mine, 2 * group + 1, peer1).wait()
    o_ref[...] = whole[...].astype(F32) * scale


def dp_sum(rows, dp, scale):
    group = dp // 4
    unit = 16 * dp
    count = -(-rows.shape[0] // unit) * unit
    rows = jnp.pad(rows, ((0, count - rows.shape[0]), (0, 0)))
    half, quarter = count // 2, count // 4
    part = quarter // group
    vmem = pl.BlockSpec(memory_space=pltpu.VMEM)

    def kernel(*refs):
        reduce_kernel(group, scale, *refs)

    return pl.pallas_call(
        kernel,
        out_shape=jax.ShapeDtypeStruct((count, LANES), F32),
        in_specs=[vmem],
        out_specs=vmem,
        scratch_shapes=[
            pltpu.VMEM((half, LANES), BF16),
            pltpu.VMEM((half, LANES), BF16),
            pltpu.VMEM((half, LANES), F32),
            pltpu.VMEM((quarter, LANES), BF16),
            pltpu.VMEM((quarter, LANES), BF16),
            pltpu.VMEM((quarter, LANES), F32),
            pltpu.VMEM((quarter, LANES), BF16),
            pltpu.VMEM((group - 1, part, LANES), BF16),
            pltpu.VMEM((count, LANES), BF16),
            pltpu.SemaphoreType.DMA((2 * group + 2,)),
            pltpu.SemaphoreType.DMA((2 * group + 2,)),
        ],
        compiler_params=pltpu.CompilerParams(
            collective_id=0, has_side_effects=True, vmem_limit_bytes=24 << 20
        ),
        cost_estimate=pl.CostEstimate(flops=0, bytes_accessed=120_000_000, transcendentals=0),
    )(rows)


def per_device(frames, gain, w_first, w_second, w_third, w_fourth, cotangent):
    n = lax.axis_size("tensor")
    dp = lax.axis_size("dp")
    a_loc, i_sz, m_sz = w_first.shape
    m_loc, a_sz, q_sz = w_second.shape
    width = a_sz * i_sz
    t_loc = frames.shape[0] // n

    x = swap_in(frames, n)
    packed = jnp.concatenate(
        [
            to_rows(w_first, 1)[0],
            to_rows(w_second, 1)[0],
            to_rows(jnp.transpose(w_third, (0, 2, 1)), 1)[0],
            to_rows(jnp.transpose(w_fourth, (0, 2, 1)), 1)[0],
            jnp.pad(gain.reshape(-1, LANES), ((0, -(gain.shape[0] // LANES) % 16), (0, 0))),
        ],
        0,
    )
    packed = lax.all_to_all(jnp.broadcast_to(packed[None], (n,) + packed.shape), "tensor", 0, 0)
    cot = swap_in(cotangent, n)

    def blocks(index, b, r, c):
        size = w_first.size // LANES
        halves = [from_rows(packed[j, index * size : (index + 1) * size], b, r, c) for j in range(n)]
        return jnp.concatenate(halves, 0)

    w1 = blocks(0, a_loc, i_sz, m_sz)
    w2 = blocks(1, m_loc, a_sz, q_sz)
    w3 = blocks(2, m_loc, a_sz, q_sz)
    w4 = blocks(3, a_loc, i_sz, m_sz)
    start = 4 * w_first.size // LANES
    gain_full = packed[:, start : start + gain.shape[0] // LANES].reshape(-1)

    xf = x.astype(F32)
    gw = gain_full.astype(F32)[:, None]
    mean = jnp.sum(xf, 0, keepdims=True) / width
    msq = jnp.sum(xf * xf, 0, keepdims=True) / width
    rstd = 1.0 / jnp.sqrt(msq - mean * mean + 1e-05)
    xhat = (xf - mean) * rstd
    normed = (xhat * gw).astype(BF16).reshape(a_sz, i_sz, t_loc)
    lifted = dot32("ait,aim->amt", normed, w1).astype(BF16)
    mixed = dot32("amt,maq->mqt", lifted, w2)
    act, slope = gelu_parts(mixed)
    act = act.astype(BF16)
    folded = dot32("mqt,mpq->mpt", act, w3).astype(BF16)
    back = dot32("mat,aim->ait", folded, w4).reshape(width, t_loc)
    output = swap_out((xf + 0.5 * back).astype(BF16), n)

    dz = (0.5 * cot.astype(F32)).astype(BF16).reshape(a_sz, i_sz, t_loc)
    g4 = to_rows(dot32("mat,ait->aim", folded, dz), n)
    dfold = dot32("ait,aim->mat", dz, w4).astype(BF16)
    g3 = to_rows(dot32("mqt,mpt->mpq", act, dfold), n)
    dmix = (dot32("mpt,mpq->mqt", dfold, w3) * slope).astype(BF16)
    g2 = to_rows(dot32("amt,mqt->maq", lifted, dmix), n)
    early = tensor_sum([g4, g3, g2], n)
    dlift = dot32("mqt,maq->amt", dmix, w2).astype(BF16)
    g1 = to_rows(dot32("ait,amt->aim", normed, dlift), n)
    dn = dot32("amt,aim->ait", dlift, w1).reshape(width, t_loc)
    gg = jnp.sum(dn * xhat, 1)
    e = dn * gw
    e_mean = jnp.sum(e, 0, keepdims=True) / width
    ex_mean = jnp.sum(e * xhat, 0, keepdims=True) / width
    dx = (cot.astype(F32) + rstd * (e - e_mean - xhat * ex_mean)).astype(BF16)
    input_gradient = swap_out(dx, n)
    late = tensor_sum([g1, gg.reshape(n, -1, LANES)], n)

    total = dp_sum(jnp.concatenate([early, late], 0), dp, 1.0 / math.sqrt(frames.shape[0] * dp))
    r = g1.shape[1]
    s4 = jnp.transpose(from_rows(total[:r], a_loc, i_sz, m_sz), (0, 2, 1))
    s3 = jnp.transpose(from_rows(total[r : 2 * r], m_loc, a_sz, q_sz), (0, 2, 1))
    s2 = from_rows(total[2 * r : 3 * r], m_loc, a_sz, q_sz)
    s1 = from_rows(total[3 * r : 4 * r], a_loc, i_sz, m_sz)
    sg = total[4 * r : 4 * r + gain.shape[0] // LANES].reshape(-1)
    return (output, input_gradient, s1, s2, s3, s4, sg)


def solution(mesh):
    blocks = P("tensor", None, None)
    rows = P("dp", "tensor")
    return jax.shard_map(
        per_device,
        mesh=mesh,
        in_specs=(rows, P("tensor"), blocks, blocks, blocks, blocks, rows),
        out_specs=(rows, rows, blocks, blocks, blocks, blocks, P("tensor")),
        check_vma=False,
    )
```

```python
import math

import jax
import jax.numpy as jnp
from jax import lax
from jax.experimental import pallas as pl
from jax.experimental.pallas import tpu as pltpu
from jax.sharding import PartitionSpec as P

F32 = jnp.float32
BF16 = jnp.bfloat16
LANES = 128


def gelu_parts(value):
    cdf = 0.5 * (1.0 + jax.scipy.special.erf(value * 0.7071067811865476))
    pdf = jnp.exp(-0.5 * value * value) * 0.3989422804014327
    return (value * cdf, cdf + value * pdf)


def dot32(spec, a, b):
    return jnp.einsum(spec, a, b, preferred_element_type=F32)


def send_parts(parts, n):
    me = lax.axis_index("tensor")
    own = lax.dynamic_index_in_dim(parts, me, 0, keepdims=False)
    got = []
    for k in range(1, n):
        chunk = lax.dynamic_index_in_dim(parts, (me + k) % n, 0, keepdims=False)
        got.append(((me + n - k) % n, lax.ppermute(chunk, "tensor", [(i, (i + k) % n) for i in range(n)])))
    return own, got


def place(own, got, n):
    result = jnp.broadcast_to(own[None], (n,) + own.shape)
    for source, part in got:
        result = lax.dynamic_update_index_in_dim(result, part, source, 0)
    return result


def swap_in(x, n):
    t, d = x.shape
    own, got = send_parts(x.reshape(n, t // n, d), n)
    return place(own.T, [(source, part.T) for source, part in got], n).reshape(n * d, t // n)


def swap_out(x, n):
    d, t = x.shape
    own, got = send_parts(x.reshape(n, d // n, t), n)
    return place(own.T, [(source, part.T) for source, part in got], n).reshape(n * t, d // n)


def to_rows(g, n):
    b, r, c = g.shape
    k = LANES // c
    g = g.reshape(n, b // n, r, c)
    step = b // n // k
    if k > 1:
        g = jnp.concatenate([g[:, i * step : (i + 1) * step] for i in range(k)], axis=-1)
    return g.reshape(n, step * r, LANES)


def from_rows(rows, b, r, c):
    k = LANES // c
    g = rows.reshape(b // k, r, LANES)
    if k > 1:
        g = jnp.concatenate([g[:, :, i * c : (i + 1) * c] for i in range(k)], axis=0)
    return g


def tensor_sum(rows, n):
    own, got = send_parts(jnp.concatenate([r.astype(BF16) for r in rows], 1), n)
    total = own.astype(F32)
    for _, part in got:
        total += part.astype(F32)
    return total


def reduce_kernel(group, scale, x_ref, o_ref, send1, recv1, acc1, send2, recv2, acc2, send3, recv3, whole, ssem, rsem):
    me = lax.axis_index("dp")
    rows = x_ref.shape[0]
    half, quarter = rows // 2, rows // 4
    part = quarter // group
    d1, d2, d3 = me % 2, (me // 2) % 2, me // 4
    peer1 = me + 1 - 2 * d1
    peer2 = me + 2 - 4 * d2
    others = [((d3 + k) % group, (d3 + group - k) % group) for k in range(1, group)]

    barrier = pltpu.get_barrier_semaphore()
    for peer in [peer1, peer2] + [to * 4 + me % 4 for to, _ in others]:
        pl.semaphore_signal(barrier, inc=1, device_id={"dp": peer}, device_id_type=pl.DeviceIdType.MESH)
    pl.semaphore_wait(barrier, 1 + group)

    def send(src, dst, slot, peer):
        copy = pltpu.make_async_remote_copy(
            src_ref=src,
            dst_ref=dst,
            send_sem=ssem.at[slot],
            recv_sem=rsem.at[slot],
            device_id={"dp": peer},
            device_id_type=pl.DeviceIdType.MESH,
        )
        copy.start()
        return copy

    def window(start, size):
        return pl.ds(pl.multiple_of(start, 16), size)

    send1[...] = x_ref[window((1 - d1) * half, half), :].astype(BF16)
    copy = send(send1, recv1, 0, peer1)
    acc1[...] = x_ref[window(d1 * half, half), :]
    copy.wait()
    acc1[...] += recv1[...].astype(F32)

    send2[...] = acc1[window((1 - d2) * quarter, quarter), :].astype(BF16)
    copy = send(send2, recv2, 1, peer2)
    acc2[...] = acc1[window(d2 * quarter, quarter), :]
    copy.wait()
    acc2[...] += recv2[...].astype(F32)

    send3[...] = acc2[...].astype(BF16)
    copies = []
    for k, (to, _) in enumerate(others):
        copies.append(send(send3.at[window(to * part, part), :], recv3.at[k], 2 + k, to * 4 + me % 4))
    total = acc2[window(d3 * part, part), :]
    for k, copy in enumerate(copies):
        copy.wait()
        total += recv3[k].astype(F32)

    base1 = d1 * half
    base2 = base1 + d2 * quarter
    base3 = base2 + d3 * part
    whole[window(base3, part), :] = total.astype(BF16)
    mine = whole.at[window(base3, part), :]
    copies = []
    for k, (to, _) in enumerate(others):
        copies.append(send(mine, mine, 1 + group + k, to * 4 + me % 4))
    for copy in copies:
        copy.wait()
    mine = whole.at[window(base2, quarter), :]
    send(mine, mine, 2 * group, peer2).wait()
    mine = whole.at[window(base1, half), :]
    send(mine, mine, 2 * group + 1, peer1).wait()
    o_ref[...] = whole[...].astype(F32) * scale


def dp_sum(rows, dp, scale):
    group = dp // 4
    unit = 16 * dp
    count = -(-rows.shape[0] // unit) * unit
    rows = jnp.pad(rows, ((0, count - rows.shape[0]), (0, 0)))
    half, quarter = count // 2, count // 4
    part = quarter // group
    vmem = pl.BlockSpec(memory_space=pltpu.VMEM)

    def kernel(*refs):
        reduce_kernel(group, scale, *refs)

    return pl.pallas_call(
        kernel,
        out_shape=jax.ShapeDtypeStruct((count, LANES), F32),
        in_specs=[vmem],
        out_specs=vmem,
        scratch_shapes=[
            pltpu.VMEM((half, LANES), BF16),
            pltpu.VMEM((half, LANES), BF16),
            pltpu.VMEM((half, LANES), F32),
            pltpu.VMEM((quarter, LANES), BF16),
            pltpu.VMEM((quarter, LANES), BF16),
            pltpu.VMEM((quarter, LANES), F32),
            pltpu.VMEM((quarter, LANES), BF16),
            pltpu.VMEM((group - 1, part, LANES), BF16),
            pltpu.VMEM((count, LANES), BF16),
            pltpu.SemaphoreType.DMA((2 * group + 2,)),
            pltpu.SemaphoreType.DMA((2 * group + 2,)),
        ],
        compiler_params=pltpu.CompilerParams(
            collective_id=0, has_side_effects=True, vmem_limit_bytes=24 << 20
        ),
        cost_estimate=pl.CostEstimate(flops=0, bytes_accessed=120_000_000, transcendentals=0),
    )(rows)


def per_device(frames, gain, w_first, w_second, w_third, w_fourth, cotangent):
    n = lax.axis_size("tensor")
    dp = lax.axis_size("dp")
    a_loc, i_sz, m_sz = w_first.shape
    m_loc, a_sz, q_sz = w_second.shape
    width = a_sz * i_sz
    t_loc = frames.shape[0] // n

    x = swap_in(frames, n)
    packed = jnp.concatenate(
        [
            to_rows(w_first, 1)[0],
            to_rows(w_second, 1)[0],
            to_rows(jnp.transpose(w_third, (0, 2, 1)), 1)[0],
            to_rows(jnp.transpose(w_fourth, (0, 2, 1)), 1)[0],
            jnp.pad(gain.reshape(-1, LANES), ((0, -(gain.shape[0] // LANES) % 16), (0, 0))),
        ],
        0,
    )
    me = lax.axis_index("tensor")
    arrived = []
    for k in range(1, n):
        part = lax.ppermute(packed, "tensor", [(i, (i + k) % n) for i in range(n)])
        arrived.append(((me + n - k) % n, part))
    packed = place(packed, arrived, n)
    cotangent, packed = lax.optimization_barrier((cotangent, packed))
    cot = swap_in(cotangent, n)

    def blocks(index, b, r, c):
        size = w_first.size // LANES
        halves = [from_rows(packed[j, index * size : (index + 1) * size], b, r, c) for j in range(n)]
        return jnp.concatenate(halves, 0)

    w1 = blocks(0, a_loc, i_sz, m_sz)
    w2 = blocks(1, m_loc, a_sz, q_sz)
    w3 = blocks(2, m_loc, a_sz, q_sz)
    w4 = blocks(3, a_loc, i_sz, m_sz)
    start = 4 * w_first.size // LANES
    gain_full = packed[:, start : start + gain.shape[0] // LANES].reshape(-1)

    xf = x.astype(F32)
    gw = gain_full.astype(F32)[:, None]
    mean = jnp.sum(xf, 0, keepdims=True) / width
    msq = jnp.sum(xf * xf, 0, keepdims=True) / width
    rstd = 1.0 / jnp.sqrt(msq - mean * mean + 1e-05)
    xhat = (xf - mean) * rstd
    normed = (xhat * gw).astype(BF16).reshape(a_sz, i_sz, t_loc)
    lifted = dot32("ait,aim->amt", normed, w1).astype(BF16)
    mixed = dot32("amt,maq->mqt", lifted, w2)
    act, slope = gelu_parts(mixed)
    act = act.astype(BF16)
    folded = dot32("mqt,mpq->mpt", act, w3).astype(BF16)
    back = dot32("mat,aim->ait", folded, w4).reshape(width, t_loc)
    output = swap_out((xf + 0.5 * back).astype(BF16), n)

    dz = (0.5 * cot.astype(F32)).astype(BF16).reshape(a_sz, i_sz, t_loc)
    g4 = to_rows(dot32("mat,ait->aim", folded, dz), n)
    dfold = dot32("ait,aim->mat", dz, w4).astype(BF16)
    g3 = to_rows(dot32("mqt,mpt->mpq", act, dfold), n)
    dmix = (dot32("mpt,mpq->mqt", dfold, w3) * slope).astype(BF16)
    g2 = to_rows(dot32("amt,mqt->maq", lifted, dmix), n)
    early = tensor_sum([g4, g3, g2], n)
    dlift = dot32("mqt,maq->amt", dmix, w2).astype(BF16)
    g1 = to_rows(dot32("ait,amt->aim", normed, dlift), n)
    dn = dot32("amt,aim->ait", dlift, w1).reshape(width, t_loc)
    gg = jnp.sum(dn * xhat, 1)
    e = dn * gw
    e_mean = jnp.sum(e, 0, keepdims=True) / width
    ex_mean = jnp.sum(e * xhat, 0, keepdims=True) / width
    dx = (cot.astype(F32) + rstd * (e - e_mean - xhat * ex_mean)).astype(BF16)
    input_gradient = swap_out(dx, n)
    late = tensor_sum([g1, gg.reshape(n, -1, LANES)], n)

    total = dp_sum(jnp.concatenate([early, late], 0), dp, 1.0 / math.sqrt(frames.shape[0] * dp))
    r = g1.shape[1]
    s4 = jnp.transpose(from_rows(total[:r], a_loc, i_sz, m_sz), (0, 2, 1))
    s3 = jnp.transpose(from_rows(total[r : 2 * r], m_loc, a_sz, q_sz), (0, 2, 1))
    s2 = from_rows(total[2 * r : 3 * r], m_loc, a_sz, q_sz)
    s1 = from_rows(total[3 * r : 4 * r], a_loc, i_sz, m_sz)
    sg = total[4 * r : 4 * r + gain.shape[0] // LANES].reshape(-1)
    return (output, input_gradient, s1, s2, s3, s4, sg)


def solution(mesh):
    blocks = P("tensor", None, None)
    rows = P("dp", "tensor")
    return jax.shard_map(
        per_device,
        mesh=mesh,
        in_specs=(rows, P("tensor"), blocks, blocks, blocks, blocks, rows),
        out_specs=(rows, rows, blocks, blocks, blocks, blocks, P("tensor")),
        check_vma=False,
    )
```

```python
import math

import jax
import jax.numpy as jnp
from jax import lax
from jax.experimental import pallas as pl
from jax.experimental.pallas import tpu as pltpu
from jax.sharding import PartitionSpec as P

F32 = jnp.float32
BF16 = jnp.bfloat16
LANES = 128


def gelu_parts(value):
    cdf = 0.5 * (1.0 + jax.scipy.special.erf(value * 0.7071067811865476))
    pdf = jnp.exp(-0.5 * value * value) * 0.3989422804014327
    return (value * cdf, cdf + value * pdf)


def dot32(spec, a, b):
    return jnp.einsum(spec, a, b, preferred_element_type=F32)


def send_parts(parts, n):
    me = lax.axis_index("tensor")
    own = lax.dynamic_index_in_dim(parts, me, 0, keepdims=False)
    got = []
    for k in range(1, n):
        chunk = lax.dynamic_index_in_dim(parts, (me + k) % n, 0, keepdims=False)
        got.append(((me + n - k) % n, lax.ppermute(chunk, "tensor", [(i, (i + k) % n) for i in range(n)])))
    return own, got


def place(own, got, n):
    result = jnp.broadcast_to(own[None], (n,) + own.shape)
    for source, part in got:
        result = lax.dynamic_update_index_in_dim(result, part, source, 0)
    return result


def swap_in(x, n):
    t, d = x.shape
    own, got = send_parts(x.reshape(n, t // n, d), n)
    return place(own.T, [(source, part.T) for source, part in got], n).reshape(n * d, t // n)


def swap_out(x, n):
    d, t = x.shape
    own, got = send_parts(x.reshape(n, d // n, t), n)
    return place(own.T, [(source, part.T) for source, part in got], n).reshape(n * t, d // n)


def to_rows(g, n):
    b, r, c = g.shape
    k = LANES // c
    g = g.reshape(n, b // n, r, c)
    step = b // n // k
    if k > 1:
        g = jnp.concatenate([g[:, i * step : (i + 1) * step] for i in range(k)], axis=-1)
    return g.reshape(n, step * r, LANES)


def from_rows(rows, b, r, c):
    k = LANES // c
    g = rows.reshape(b // k, r, LANES)
    if k > 1:
        g = jnp.concatenate([g[:, :, i * c : (i + 1) * c] for i in range(k)], axis=0)
    return g


def pack(rows):
    return jnp.concatenate([r.astype(BF16) for r in rows], 1)


def tensor_sum(rows, n):
    own, got = send_parts(rows, n)
    total = own.astype(F32)
    for _, part in got:
        total += part.astype(F32)
    return total


def reduce_kernel(group, scale, chunks, x_ref, o_ref, *refs):
    ssem, rsem = refs[-2:]
    me = lax.axis_index("dp")
    d1, d2, d3 = me % 2, (me // 2) % 2, me // 4
    peer1 = me + 1 - 2 * d1
    peer2 = me + 2 - 4 * d2
    others = [(d3 + k) % group for k in range(1, group)]

    barrier = pltpu.get_barrier_semaphore()
    for peer in [peer1, peer2] + [to * 4 + me % 4 for to in others]:
        pl.semaphore_signal(barrier, inc=1, device_id={"dp": peer}, device_id_type=pl.DeviceIdType.MESH)
    pl.semaphore_wait(barrier, 1 + group)

    def send(src, dst, slot, peer):
        copy = pltpu.make_async_remote_copy(
            src_ref=src,
            dst_ref=dst,
            send_sem=ssem.at[slot],
            recv_sem=rsem.at[slot],
            device_id={"dp": peer},
            device_id_type=pl.DeviceIdType.MESH,
        )
        copy.start()
        return copy

    def window(start, size):
        return pl.ds(pl.multiple_of(start, 16), size)

    def run(first, rows, slot, send1, recv1, acc1, send2, recv2, acc2, send3, recv3, whole):
        half, quarter = rows // 2, rows // 4
        part = quarter // group
        send1[...] = x_ref[window(first + (1 - d1) * half, half), :].astype(BF16)
        copy = send(send1, recv1, slot, peer1)
        acc1[...] = x_ref[window(first + d1 * half, half), :]
        yield
        copy.wait()
        acc1[...] += recv1[...].astype(F32)

        send2[...] = acc1[window((1 - d2) * quarter, quarter), :].astype(BF16)
        copy = send(send2, recv2, slot + 1, peer2)
        acc2[...] = acc1[window(d2 * quarter, quarter), :]
        yield
        copy.wait()
        acc2[...] += recv2[...].astype(F32)

        send3[...] = acc2[...].astype(BF16)
        copies = []
        for k, to in enumerate(others):
            copies.append(send(send3.at[window(to * part, part), :], recv3.at[k], slot + 2 + k, to * 4 + me % 4))
        yield
        total = acc2[window(d3 * part, part), :]
        for k, copy in enumerate(copies):
            copy.wait()
            total += recv3[k].astype(F32)

        base1 = d1 * half
        base2 = base1 + d2 * quarter
        base3 = base2 + d3 * part
        whole[window(base3, part), :] = total.astype(BF16)
        mine = whole.at[window(base3, part), :]
        copies = []
        for k, to in enumerate(others):
            copies.append(send(mine, mine, slot + 1 + group + k, to * 4 + me % 4))
        yield
        for copy in copies:
            copy.wait()
        mine = whole.at[window(base2, quarter), :]
        copy = send(mine, mine, slot + 2 * group, peer2)
        yield
        copy.wait()
        mine = whole.at[window(base1, half), :]
        copy = send(mine, mine, slot + 2 * group + 1, peer1)
        yield
        copy.wait()
        o_ref[pl.ds(first, rows), :] = whole[...].astype(F32) * scale

    runs = []
    first = 0
    for c, rows in enumerate(chunks):
        runs.append(run(first, rows, c * (2 * group + 2), *refs[9 * c : 9 * c + 9]))
        first += rows
    while runs:
        runs = [r for r in runs if next(r, True) is None]


def dp_sum(rows, dp, scale):
    group = dp // 4
    unit = 16 * dp
    units = -(-rows.shape[0] // unit)
    count = units * unit
    rows = jnp.pad(rows, ((0, count - rows.shape[0]), (0, 0)))
    chunks = [u * unit for u in (units - units // 2, units // 2) if u]
    vmem = pl.BlockSpec(memory_space=pltpu.VMEM)
    scratch = []
    for size in chunks:
        half, quarter = size // 2, size // 4
        scratch += [
            pltpu.VMEM((half, LANES), BF16),
            pltpu.VMEM((half, LANES), BF16),
            pltpu.VMEM((half, LANES), F32),
            pltpu.VMEM((quarter, LANES), BF16),
            pltpu.VMEM((quarter, LANES), BF16),
            pltpu.VMEM((quarter, LANES), F32),
            pltpu.VMEM((quarter, LANES), BF16),
            pltpu.VMEM((group - 1, quarter // group, LANES), BF16),
            pltpu.VMEM((size, LANES), BF16),
        ]
    slots = len(chunks) * (2 * group + 2)

    def kernel(*refs):
        reduce_kernel(group, scale, chunks, *refs)

    return pl.pallas_call(
        kernel,
        out_shape=jax.ShapeDtypeStruct((count, LANES), F32),
        in_specs=[vmem],
        out_specs=vmem,
        scratch_shapes=scratch + [pltpu.SemaphoreType.DMA((slots,)), pltpu.SemaphoreType.DMA((slots,))],
        compiler_params=pltpu.CompilerParams(
            collective_id=0, has_side_effects=True, vmem_limit_bytes=24 << 20
        ),
        cost_estimate=pl.CostEstimate(flops=0, bytes_accessed=120_000_000, transcendentals=0),
    )(rows)


def per_device(frames, gain, w_first, w_second, w_third, w_fourth, cotangent):
    n = lax.axis_size("tensor")
    dp = lax.axis_size("dp")
    a_loc, i_sz, m_sz = w_first.shape
    m_loc, a_sz, q_sz = w_second.shape
    width = a_sz * i_sz
    t_loc = frames.shape[0] // n

    x = swap_in(frames, n)
    me = lax.axis_index("tensor")

    def gather(packed):
        arrived = []
        for k in range(1, n):
            part = lax.ppermute(packed, "tensor", [(i, (i + k) % n) for i in range(n)])
            arrived.append(((me + n - k) % n, part))
        return place(packed, arrived, n)

    first = gather(
        jnp.concatenate(
            [
                to_rows(w_first, 1)[0],
                to_rows(w_second, 1)[0],
                jnp.pad(gain.reshape(-1, LANES), ((0, -(gain.shape[0] // LANES) % 16), (0, 0))),
            ],
            0,
        )
    )
    second = jnp.concatenate(
        [
            to_rows(jnp.transpose(w_third, (0, 2, 1)), 1)[0],
            to_rows(jnp.transpose(w_fourth, (0, 2, 1)), 1)[0],
        ],
        0,
    )
    cotangent, second, first = lax.optimization_barrier((cotangent, second, first))
    second = gather(second)
    cot = swap_in(cotangent, n)

    size = w_first.size // LANES

    def blocks(packed, index, b, r, c):
        halves = [from_rows(packed[j, index * size : (index + 1) * size], b, r, c) for j in range(n)]
        return jnp.concatenate(halves, 0)

    w1 = blocks(first, 0, a_loc, i_sz, m_sz)
    w2 = blocks(first, 1, m_loc, a_sz, q_sz)
    w3 = blocks(second, 0, m_loc, a_sz, q_sz)
    w4 = blocks(second, 1, a_loc, i_sz, m_sz)
    gain_full = first[:, 2 * size : 2 * size + gain.shape[0] // LANES].reshape(-1)

    xf = x.astype(F32)
    gw = gain_full.astype(F32)[:, None]
    mean = jnp.sum(xf, 0, keepdims=True) / width
    msq = jnp.sum(xf * xf, 0, keepdims=True) / width
    rstd = 1.0 / jnp.sqrt(msq - mean * mean + 1e-05)
    xhat = (xf - mean) * rstd
    normed = (xhat * gw).astype(BF16).reshape(a_sz, i_sz, t_loc)
    lifted = dot32("ait,aim->amt", normed, w1).astype(BF16)
    mixed = dot32("amt,maq->mqt", lifted, w2)
    act, slope = gelu_parts(mixed)
    act = act.astype(BF16)
    folded = dot32("mqt,mpq->mpt", act, w3).astype(BF16)
    back = dot32("mat,aim->ait", folded, w4).reshape(width, t_loc)
    output, cot = lax.optimization_barrier(((xf + 0.5 * back).astype(BF16), cot))
    output = swap_out(output, n)

    dz = (0.5 * cot.astype(F32)).astype(BF16).reshape(a_sz, i_sz, t_loc)
    g4 = to_rows(dot32("mat,ait->aim", folded, dz), n)
    dfold = dot32("ait,aim->mat", dz, w4).astype(BF16)
    g3 = to_rows(dot32("mqt,mpt->mpq", act, dfold), n)
    dmix = (dot32("mpt,mpq->mqt", dfold, w3) * slope).astype(BF16)
    g2 = to_rows(dot32("amt,mqt->maq", lifted, dmix), n)
    dlift = dot32("mqt,maq->amt", dmix, w2).astype(BF16)
    early, dlift = lax.optimization_barrier((pack([g4, g3, g2]), dlift))
    early = tensor_sum(early, n)
    g1 = to_rows(dot32("ait,amt->aim", normed, dlift), n)
    dn = dot32("amt,aim->ait", dlift, w1).reshape(width, t_loc)
    gg = jnp.sum(dn * xhat, 1)
    e = dn * gw
    e_mean = jnp.sum(e, 0, keepdims=True) / width
    ex_mean = jnp.sum(e * xhat, 0, keepdims=True) / width
    dx = (cot.astype(F32) + rstd * (e - e_mean - xhat * ex_mean)).astype(BF16)
    input_gradient = swap_out(dx, n)
    late = tensor_sum(pack([g1, gg.reshape(n, -1, LANES)]), n)

    total = dp_sum(jnp.concatenate([early, late], 0), dp, 1.0 / math.sqrt(frames.shape[0] * dp))
    r = g1.shape[1]
    s4 = jnp.transpose(from_rows(total[:r], a_loc, i_sz, m_sz), (0, 2, 1))
    s3 = jnp.transpose(from_rows(total[r : 2 * r], m_loc, a_sz, q_sz), (0, 2, 1))
    s2 = from_rows(total[2 * r : 3 * r], m_loc, a_sz, q_sz)
    s1 = from_rows(total[3 * r : 4 * r], a_loc, i_sz, m_sz)
    sg = total[4 * r : 4 * r + gain.shape[0] // LANES].reshape(-1)
    return (output, input_gradient, s1, s2, s3, s4, sg)


def solution(mesh):
    blocks = P("tensor", None, None)
    rows = P("dp", "tensor")
    return jax.shard_map(
        per_device,
        mesh=mesh,
        in_specs=(rows, P("tensor"), blocks, blocks, blocks, blocks, rows),
        out_specs=(rows, rows, blocks, blocks, blocks, blocks, P("tensor")),
        check_vma=False,
    )
```

```python
import math

import jax
import jax.numpy as jnp
from jax import lax
from jax.experimental import pallas as pl
from jax.experimental.pallas import tpu as pltpu
from jax.sharding import PartitionSpec as P

F32 = jnp.float32
BF16 = jnp.bfloat16
LANES = 128


def gelu_parts(value):
    cdf = 0.5 * (1.0 + jax.scipy.special.erf(value * 0.7071067811865476))
    pdf = jnp.exp(-0.5 * value * value) * 0.3989422804014327
    return (value * cdf, cdf + value * pdf)


def dot32(spec, a, b):
    return jnp.einsum(spec, a, b, preferred_element_type=F32)


def send_parts(parts, n):
    me = lax.axis_index("tensor")
    own = lax.dynamic_index_in_dim(parts, me, 0, keepdims=False)
    got = []
    for k in range(1, n):
        chunk = lax.dynamic_index_in_dim(parts, (me + k) % n, 0, keepdims=False)
        got.append(((me + n - k) % n, lax.ppermute(chunk, "tensor", [(i, (i + k) % n) for i in range(n)])))
    return own, got


def place(own, got, n):
    result = jnp.broadcast_to(own[None], (n,) + own.shape)
    for source, part in got:
        result = lax.dynamic_update_index_in_dim(result, part, source, 0)
    return result


def swap_in(x, n):
    t, d = x.shape
    own, got = send_parts(x.reshape(n, t // n, d), n)
    return place(own.T, [(source, part.T) for source, part in got], n).reshape(n * d, t // n)


def swap_out(x, n):
    d, t = x.shape
    own, got = send_parts(x.reshape(n, d // n, t), n)
    return place(own.T, [(source, part.T) for source, part in got], n).reshape(n * t, d // n)


def to_rows(g, n):
    b, r, c = g.shape
    k = LANES // c
    g = g.reshape(n, b // n, r, c)
    step = b // n // k
    if k > 1:
        g = jnp.concatenate([g[:, i * step : (i + 1) * step] for i in range(k)], axis=-1)
    return g.reshape(n, step * r, LANES)


def from_rows(rows, b, r, c):
    k = LANES // c
    g = rows.reshape(b // k, r, LANES)
    if k > 1:
        g = jnp.concatenate([g[:, :, i * c : (i + 1) * c] for i in range(k)], axis=0)
    return g


def pack(rows):
    return jnp.concatenate([r.astype(BF16) for r in rows], 1)


def tensor_sum(rows, n):
    own, got = send_parts(rows, n)
    total = own.astype(F32)
    for _, part in got:
        total += part.astype(F32)
    return total


def reduce_kernel(group, scale, chunks, x_ref, o_ref, *refs):
    ssem, rsem = refs[-2:]
    me = lax.axis_index("dp")
    d1, d2, d3 = me % 2, (me // 2) % 2, me // 4
    peer1 = me + 1 - 2 * d1
    peer2 = me + 2 - 4 * d2
    others = [(d3 + k) % group for k in range(1, group)]

    barrier = pltpu.get_barrier_semaphore()
    for peer in [peer1, peer2] + [to * 4 + me % 4 for to in others]:
        pl.semaphore_signal(barrier, inc=1, device_id={"dp": peer}, device_id_type=pl.DeviceIdType.MESH)
    pl.semaphore_wait(barrier, 1 + group)

    def send(src, dst, slot, peer):
        copy = pltpu.make_async_remote_copy(
            src_ref=src,
            dst_ref=dst,
            send_sem=ssem.at[slot],
            recv_sem=rsem.at[slot],
            device_id={"dp": peer},
            device_id_type=pl.DeviceIdType.MESH,
        )
        copy.start()
        return copy

    def window(start, size):
        return pl.ds(pl.multiple_of(start, 16), size)

    def run(first, rows, slot, send1, recv1, acc1, send2, recv2, acc2, send3, recv3, whole):
        half, quarter = rows // 2, rows // 4
        part = quarter // group
        send1[...] = x_ref[window(first + (1 - d1) * half, half), :].astype(BF16)
        copy = send(send1, recv1, slot, peer1)
        acc1[...] = x_ref[window(first + d1 * half, half), :]
        yield
        copy.wait()
        acc1[...] += recv1[...].astype(F32)

        send2[...] = acc1[window((1 - d2) * quarter, quarter), :].astype(BF16)
        copy = send(send2, recv2, slot + 1, peer2)
        acc2[...] = acc1[window(d2 * quarter, quarter), :]
        yield
        copy.wait()
        acc2[...] += recv2[...].astype(F32)

        send3[...] = acc2[...].astype(BF16)
        copies = []
        for k, to in enumerate(others):
            copies.append(send(send3.at[window(to * part, part), :], recv3.at[k], slot + 2 + k, to * 4 + me % 4))
        yield
        total = acc2[window(d3 * part, part), :]
        for k, copy in enumerate(copies):
            copy.wait()
            total += recv3[k].astype(F32)

        base1 = d1 * half
        base2 = base1 + d2 * quarter
        base3 = base2 + d3 * part
        whole[window(base3, part), :] = total.astype(BF16)
        mine = whole.at[window(base3, part), :]
        copies = []
        for k, to in enumerate(others):
            copies.append(send(mine, mine, slot + 1 + group + k, to * 4 + me % 4))
        yield
        for copy in copies:
            copy.wait()
        mine = whole.at[window(base2, quarter), :]
        copy = send(mine, mine, slot + 2 * group, peer2)
        yield
        copy.wait()
        mine = whole.at[window(base1, half), :]
        copy = send(mine, mine, slot + 2 * group + 1, peer1)
        yield
        copy.wait()
        o_ref[pl.ds(first, rows), :] = whole[...].astype(F32) * scale

    runs = []
    first = 0
    for c, rows in enumerate(chunks):
        runs.append(run(first, rows, c * (2 * group + 2), *refs[9 * c : 9 * c + 9]))
        first += rows
    while runs:
        runs = [r for r in runs if next(r, True) is None]


def dp_sum(rows, dp, scale):
    group = dp // 4
    unit = 16 * dp
    units = -(-rows.shape[0] // unit)
    count = units * unit
    rows = jnp.pad(rows, ((0, count - rows.shape[0]), (0, 0)))
    chunks = [u * unit for u in (units - units // 2, units // 2) if u]
    vmem = pl.BlockSpec(memory_space=pltpu.VMEM)
    scratch = []
    for size in chunks:
        half, quarter = size // 2, size // 4
        scratch += [
            pltpu.VMEM((half, LANES), BF16),
            pltpu.VMEM((half, LANES), BF16),
            pltpu.VMEM((half, LANES), F32),
            pltpu.VMEM((quarter, LANES), BF16),
            pltpu.VMEM((quarter, LANES), BF16),
            pltpu.VMEM((quarter, LANES), F32),
            pltpu.VMEM((quarter, LANES), BF16),
            pltpu.VMEM((group - 1, quarter // group, LANES), BF16),
            pltpu.VMEM((size, LANES), BF16),
        ]
    slots = len(chunks) * (2 * group + 2)

    def kernel(*refs):
        reduce_kernel(group, scale, chunks, *refs)

    return pl.pallas_call(
        kernel,
        out_shape=jax.ShapeDtypeStruct((count, LANES), F32),
        in_specs=[vmem],
        out_specs=vmem,
        scratch_shapes=scratch + [pltpu.SemaphoreType.DMA((slots,)), pltpu.SemaphoreType.DMA((slots,))],
        compiler_params=pltpu.CompilerParams(
            collective_id=0, has_side_effects=True, vmem_limit_bytes=24 << 20
        ),
        cost_estimate=pl.CostEstimate(flops=0, bytes_accessed=120_000_000, transcendentals=0),
    )(rows)


def per_device(frames, gain, w_first, w_second, w_third, w_fourth, cotangent):
    n = lax.axis_size("tensor")
    dp = lax.axis_size("dp")
    a_loc, i_sz, m_sz = w_first.shape
    m_loc, a_sz, q_sz = w_second.shape
    width = a_sz * i_sz
    t_loc = frames.shape[0] // n

    x = swap_in(frames, n)
    me = lax.axis_index("tensor")

    def gather(packed):
        arrived = []
        for k in range(1, n):
            part = lax.ppermute(packed, "tensor", [(i, (i + k) % n) for i in range(n)])
            arrived.append(((me + n - k) % n, part))
        return place(packed, arrived, n)

    first = gather(
        jnp.concatenate(
            [
                to_rows(w_first, 1)[0],
                to_rows(w_second, 1)[0],
                jnp.pad(gain.reshape(-1, LANES), ((0, -(gain.shape[0] // LANES) % 16), (0, 0))),
            ],
            0,
        )
    )
    second = jnp.concatenate(
        [
            to_rows(jnp.transpose(w_third, (0, 2, 1)), 1)[0],
            to_rows(jnp.transpose(w_fourth, (0, 2, 1)), 1)[0],
        ],
        0,
    )
    second, first = lax.optimization_barrier((second, first))
    cotangent, x = lax.optimization_barrier((cotangent, x))
    second = gather(second)
    cot = swap_in(cotangent, n)

    size = w_first.size // LANES

    def blocks(packed, index, b, r, c):
        halves = [from_rows(packed[j, index * size : (index + 1) * size], b, r, c) for j in range(n)]
        return jnp.concatenate(halves, 0)

    w1 = blocks(first, 0, a_loc, i_sz, m_sz)
    w2 = blocks(first, 1, m_loc, a_sz, q_sz)
    w3 = blocks(second, 0, m_loc, a_sz, q_sz)
    w4 = blocks(second, 1, a_loc, i_sz, m_sz)
    gain_full = first[:, 2 * size : 2 * size + gain.shape[0] // LANES].reshape(-1)

    xf = x.astype(F32)
    gw = gain_full.astype(F32)[:, None]
    mean = jnp.sum(xf, 0, keepdims=True) / width
    msq = jnp.sum(xf * xf, 0, keepdims=True) / width
    rstd = 1.0 / jnp.sqrt(msq - mean * mean + 1e-05)
    xhat = (xf - mean) * rstd
    normed = (xhat * gw).astype(BF16).reshape(a_sz, i_sz, t_loc)
    lifted = dot32("ait,aim->amt", normed, w1).astype(BF16)
    mixed = dot32("amt,maq->mqt", lifted, w2)
    act, slope = gelu_parts(mixed)
    act = act.astype(BF16)
    folded = dot32("mqt,mpq->mpt", act, w3).astype(BF16)
    back = dot32("mat,aim->ait", folded, w4).reshape(width, t_loc)
    output, cot = lax.optimization_barrier(((xf + 0.5 * back).astype(BF16), cot))
    output = swap_out(output, n)

    dz = (0.5 * cot.astype(F32)).astype(BF16).reshape(a_sz, i_sz, t_loc)
    g4 = to_rows(dot32("mat,ait->aim", folded, dz), n)
    dfold = dot32("ait,aim->mat", dz, w4).astype(BF16)
    g3 = to_rows(dot32("mqt,mpt->mpq", act, dfold), n)
    dmix = (dot32("mpt,mpq->mqt", dfold, w3) * slope).astype(BF16)
    g2 = to_rows(dot32("amt,mqt->maq", lifted, dmix), n)
    dlift = dot32("mqt,maq->amt", dmix, w2).astype(BF16)
    early, dlift, output = lax.optimization_barrier((pack([g4, g3, g2]), dlift, output))
    early = tensor_sum(early, n)
    g1 = to_rows(dot32("ait,amt->aim", normed, dlift), n)
    dn = dot32("amt,aim->ait", dlift, w1).reshape(width, t_loc)
    gg = jnp.sum(dn * xhat, 1)
    e = dn * gw
    e_mean = jnp.sum(e, 0, keepdims=True) / width
    ex_mean = jnp.sum(e * xhat, 0, keepdims=True) / width
    early, e_mean, ex_mean, gg = lax.optimization_barrier((early, e_mean, ex_mean, gg))
    dx = (cot.astype(F32) + rstd * (e - e_mean - xhat * ex_mean)).astype(BF16)
    input_gradient = swap_out(dx, n)
    late = tensor_sum(pack([g1, gg.reshape(n, -1, LANES)]), n)

    total = dp_sum(jnp.concatenate([early, late], 0), dp, 1.0 / math.sqrt(frames.shape[0] * dp))
    r = g1.shape[1]
    s4 = jnp.transpose(from_rows(total[:r], a_loc, i_sz, m_sz), (0, 2, 1))
    s3 = jnp.transpose(from_rows(total[r : 2 * r], m_loc, a_sz, q_sz), (0, 2, 1))
    s2 = from_rows(total[2 * r : 3 * r], m_loc, a_sz, q_sz)
    s1 = from_rows(total[3 * r : 4 * r], a_loc, i_sz, m_sz)
    sg = total[4 * r : 4 * r + gain.shape[0] // LANES].reshape(-1)
    return (output, input_gradient, s1, s2, s3, s4, sg)


def solution(mesh):
    blocks = P("tensor", None, None)
    rows = P("dp", "tensor")
    return jax.shard_map(
        per_device,
        mesh=mesh,
        in_specs=(rows, P("tensor"), blocks, blocks, blocks, blocks, rows),
        out_specs=(rows, rows, blocks, blocks, blocks, blocks, P("tensor")),
        check_vma=False,
    )
```
